32 devices in a mesh: dp: 4 (over y, core), fsdp: 8 (over z, x).
Axes of the slice: x: 2, y: 2, z: 4, core: 2. Of those that a mesh axis runs over, the one named last changes fastest.
Arguments:
- hidden_in: bfloat16 [32, 192, 960], P(('dp', 'fsdp')), may hold values from -6 to 6
- cotangent: bfloat16 [32, 192, 960], P(('dp', 'fsdp')), may hold values from -6 to 6
- segment_ids: int32 [32, 192], P(('dp', 'fsdp')), may hold values from 0 to 5, never falling along the last dimension, each value on 1 to 96 neighbouring positions
- w_query: bfloat16 [960, 960], P('fsdp'), may hold values from -0.1875 to 0.1875
- w_key: bfloat16 [960, 320], P('fsdp'), may hold values from -0.1875 to 0.1875
- w_value: bfloat16 [960, 320], P('fsdp'), may hold values from -0.1875 to 0.1875
- w_output: bfloat16 [960, 960], P(None, 'fsdp'), may hold values from -0.75 to 0.75
- w_gate: bfloat16 [960, 2560], P('fsdp'), may hold values from -0.1875 to 0.1875
- w_up: bfloat16 [960, 2560], P('fsdp'), may hold values from -0.1875 to 0.1875
- w_down: bfloat16 [2560, 960], P('fsdp'), may hold values from -0.125 to 0.125
- gain_attn: bfloat16 [960], P('fsdp'), may hold values from 0.5 to 1.5
- gain_ffn: bfloat16 [960], P('fsdp'), may hold values from 0.5 to 1.5
Outputs:
- hidden_out: bfloat16 [32, 192, 960], P(('dp', 'fsdp'))
- grad_in: float32 [32, 192, 960], P(('dp', 'fsdp'))
- grad_query: float32 [960, 960], P('fsdp')
- grad_key: float32 [960, 320], P('fsdp')
- grad_value: float32 [960, 320], P('fsdp')
- grad_output: float32 [960, 960], P(None, 'fsdp')
- grad_gate: float32 [960, 2560], P('fsdp')
- grad_up: float32 [960, 2560], P('fsdp')
- grad_down: float32 [2560, 960], P('fsdp')
- grad_gain_attn: float32 [960], P('fsdp')
- grad_gain_ffn: float32 [960], P('fsdp')
The draws below stay inside these ranges and needn't reach their ends.
All inputs are finite; a program needn't handle non-finite values.
Results may differ from the reference program's by a relative error of at most 0.013.
Values may be sent and summed in bfloat16 or wider, within the bound.
No kernel may reach another device: no remote copies, remote signals or barrier semaphores. Data moves between devices by JAX's collectives and lax.ppermute only.
A program may use at most 192 MiB of HBM per device.

```python
import math
import jax
import jax.numpy as jnp
import numpy as np
from jax import lax

D = 960
FF = 2560
HQ = 15
HK = 5
HD = 64
TOK_DEV = 192
PACKS = 32


def levels(stream_key, extent, pieces, smallest, top_value):
    factor_of, own = 1.0, jax.random.fold_in(stream_key, 6)
    for dim, blocks in pieces:
        draws = jnp.exp(jax.random.uniform(jax.random.fold_in(own, dim), (blocks,), jnp.float32, smallest / len(pieces), top_value / len(pieces)))
        factor_of = factor_of * jnp.repeat(draws, extent[dim] // blocks).reshape([-1 if axis == dim else 1 for axis in range(len(extent))])
    return factor_of


def length_profile(number_of, total, limit, slope):
    loads = [(1 << 20) // math.isqrt(grade ** slope) + 1 for grade in range(2, number_of + 1)]
    surplus, holding = total - limit - (number_of - 1), [1] * (number_of - 1)
    while surplus > 0:
        movable = [i for i in range(number_of - 1) if holding[i] < limit]
        pool, remaining = sum([loads[i] for i in movable]), surplus
        for i in movable:
            extra = min(limit - holding[i], max(1, remaining * loads[i] // pool), surplus)
            holding[i] = holding[i] + extra
            surplus = surplus - extra
    return np.array([limit] + holding)


def uneven(own_key, amount, total, most, lean):
    if amount == 2:
        one = jax.random.randint(own_key, (), max(1, total - most), min(most, total - 1) + 1)
        return jnp.stack([one, total - one])
    sizes = jnp.asarray(length_profile(amount, total, most, lean), jnp.int32)
    pairs = (amount - 1) // 2
    giver, taker = sizes[1:1 + 2 * pairs:2], sizes[2:2 + 2 * pairs:2]
    margin = jnp.minimum(giver - 1, most - taker)
    shifted = jax.random.randint(jax.random.fold_in(own_key, 1), (pairs,), 0, 1 << 20) % (margin + 1)
    sizes = sizes.at[1:1 + 2 * pairs:2].set(giver - shifted).at[2:2 + 2 * pairs:2].set(taker + shifted)
    return sizes[jax.random.permutation(jax.random.fold_in(own_key, 2), amount)]


def scatter_about(key, shape, spread, limit, shards=(), kind=jnp.bfloat16):
    values = spread * jax.random.normal(key, shape, jnp.float32)
    if shards:
        values = values * levels(key, shape, shards, -0.22, 0.18)
    return jnp.clip(values, -limit, limit).astype(kind)


def setup_inputs(seed: int = 0) -> dict:
    arg_keys = jax.random.split(jax.random.key(seed), 13)
    return {
        "hidden_in": scatter_about(arg_keys[0], (PACKS, TOK_DEV, D), 1.0, 6.0, ((0, 32),)),
        "cotangent": scatter_about(arg_keys[1], (PACKS, TOK_DEV, D), 1.0, 6.0, ((0, 32),)),
        "segment_ids": jax.vmap(lambda own: jnp.searchsorted(jnp.cumsum(uneven(own, max(4, TOK_DEV // 32), TOK_DEV, TOK_DEV // 2, 2)), jnp.arange(TOK_DEV), side="right"))(jax.random.split(arg_keys[2], PACKS)).reshape((PACKS, TOK_DEV)).astype(jnp.int32),
        "w_query": scatter_about(arg_keys[3], (D, HQ * HD), D ** -0.5, 0.1875, ((0, 8),)),
        "w_key": scatter_about(arg_keys[4], (D, HK * HD), D ** -0.5, 0.1875, ((0, 8),)),
        "w_value": scatter_about(arg_keys[5], (D, HK * HD), D ** -0.5, 0.1875, ((0, 8),)),
        "w_output": scatter_about(arg_keys[6], (HQ * HD, D), (HQ * HD // 16) ** -0.5, 0.75, ((1, 8),)),
        "w_gate": scatter_about(arg_keys[7], (D, FF), D ** -0.5, 0.1875, ((0, 8),)),
        "w_up": scatter_about(arg_keys[8], (D, FF), D ** -0.5, 0.1875, ((0, 8),)),
        "w_down": scatter_about(arg_keys[9], (FF, D), FF ** -0.5, 0.125, ((0, 8),)),
        "gain_attn": jnp.clip(1.0 + 0.1 * jax.random.normal(arg_keys[10], (D,), jnp.float32), 0.5, 1.5).astype(jnp.bfloat16),
        "gain_ffn": jnp.clip(1.0 + 0.1 * jax.random.normal(arg_keys[11], (D,), jnp.float32), 0.5, 1.5).astype(jnp.bfloat16),
    }


EPS = 1e-05
THETA = 100000.0

def multiply(form, left, right):
    return jnp.einsum(form, left.astype(jnp.float32), right.astype(jnp.float32))

def tables(segments):
    count = segments.shape[0]
    index = jnp.arange(count, dtype=jnp.int32)
    same = segments[None, :] == segments[:, None]
    earlier = same & (index[None, :] < index[:, None])
    position = lax.optimization_barrier(jnp.sum(earlier.astype(jnp.float32), axis=1))
    freqs = THETA ** (-jnp.arange(HD // 2).astype(jnp.float32) * 2.0 / HD)
    angle = position[:, None] * freqs[None, :]
    visible = same & (index[None, :] <= index[:, None])
    return (jnp.cos(angle), jnp.sin(angle), visible)

def rotate(field, cosine, sine):
    half = field.shape[-1] // 2
    first, second = (field[..., :half], field[..., half:])
    cosine, sine = (cosine[:, None, :], sine[:, None, :])
    return jnp.concatenate([first * cosine - second * sine, second * cosine + first * sine], axis=-1)

def unrotate(field, cosine, sine):
    half = field.shape[-1] // 2
    first, second = (field[..., :half], field[..., half:])
    cosine, sine = (cosine[:, None, :], sine[:, None, :])
    return jnp.concatenate([first * cosine + second * sine, second * cosine - first * sine], axis=-1)

def scores_of(query_rot, key_rot, visible):
    count = query_rot.shape[0]
    grouped = query_rot.reshape(count, HK, HQ // HK, HD)
    scores = multiply('qkgd,skd->kgqs', grouped, key_rot) * HD ** (-0.5)
    return (jnp.where(visible[None, None], scores, -1e+30), grouped)

def forward(tokens, segments, weights):
    w_query, w_key, w_value, w_output, w_gate, w_up, w_down, gain_attn, gain_ffn = weights
    count = tokens.shape[0]
    base = tokens.astype(jnp.float32)
    scale_one = lax.rsqrt(lax.optimization_barrier(jnp.mean(base * base, axis=1, keepdims=True)) + EPS)
    normed_one = (base * scale_one * gain_attn.astype(jnp.float32)).astype(jnp.bfloat16)
    query = jnp.dot(normed_one, w_query, preferred_element_type=jnp.float32).reshape(count, HQ, HD)
    key = jnp.dot(normed_one, w_key, preferred_element_type=jnp.float32).reshape(count, HK, HD)
    value = jnp.dot(normed_one, w_value, preferred_element_type=jnp.float32).reshape(count, HK, HD)
    cosine, sine, visible = tables(segments)
    query_rot = rotate(query, cosine, sine).astype(jnp.bfloat16)
    key_rot = rotate(key, cosine, sine).astype(jnp.bfloat16)
    value_b = value.astype(jnp.bfloat16)
    scores, grouped = scores_of(query_rot, key_rot, visible)
    top = lax.optimization_barrier(jnp.max(scores, axis=-1, keepdims=True))
    expo = jnp.exp(scores - top)
    total = lax.optimization_barrier(jnp.sum(expo, axis=-1, keepdims=True))
    log_total = top + jnp.log(total)
    probs = (expo / total).astype(jnp.bfloat16)
    attended = multiply('kgqs,skd->qkgd', probs, value_b).reshape(count, HQ * HD).astype(jnp.bfloat16)
    mid = base + jnp.dot(attended, w_output, preferred_element_type=jnp.float32)
    scale_two = lax.rsqrt(lax.optimization_barrier(jnp.mean(mid * mid, axis=1, keepdims=True)) + EPS)
    normed_two = (mid * scale_two * gain_ffn.astype(jnp.float32)).astype(jnp.bfloat16)
    gate_pre = jnp.dot(normed_two, w_gate, preferred_element_type=jnp.float32)
    up_pre = jnp.dot(normed_two, w_up, preferred_element_type=jnp.float32)
    mixed = (gate_pre * jax.nn.sigmoid(gate_pre) * up_pre).astype(jnp.bfloat16)
    result = (mid + jnp.dot(mixed, w_down, preferred_element_type=jnp.float32)).astype(jnp.bfloat16)
    saved = (base, scale_one, normed_one, query_rot, key_rot, value_b, attended, log_total, mid, scale_two, normed_two, gate_pre, up_pre, mixed, cosine, sine, visible)
    return (result, saved)

def backward(upstream, saved, weights):
    w_query, w_key, w_value, w_output, w_gate, w_up, w_down, gain_attn, gain_ffn = weights
    base, scale_one, normed_one, query_rot, key_rot, value_b, attended, log_total, mid, scale_two, normed_two, gate_pre, up_pre, mixed, cosine, sine, visible = saved
    count = base.shape[0]
    up32 = upstream.astype(jnp.float32)
    d_mixed = jnp.dot(upstream, w_down.T, preferred_element_type=jnp.float32)
    g_down = jnp.dot(mixed.T, upstream, preferred_element_type=jnp.float32)
    sigma = jax.nn.sigmoid(gate_pre)
    d_gate = (d_mixed * up_pre * sigma * (1.0 + gate_pre * (1.0 - sigma))).astype(jnp.bfloat16)
    d_up = (d_mixed * gate_pre * sigma).astype(jnp.bfloat16)
    g_gate = jnp.dot(normed_two.T, d_gate, preferred_element_type=jnp.float32)
    g_up = jnp.dot(normed_two.T, d_up, preferred_element_type=jnp.float32)
    d_normed_two = jnp.dot(d_gate, w_gate.T, preferred_element_type=jnp.float32) + jnp.dot(d_up, w_up.T, preferred_element_type=jnp.float32)
    mid_n = mid * scale_two
    g_gain_ffn = lax.optimization_barrier(jnp.sum(d_normed_two * mid_n, axis=0))
    scaled_two = d_normed_two * gain_ffn.astype(jnp.float32)
    d_mid = up32 + scale_two * (scaled_two - mid_n * lax.optimization_barrier(jnp.mean(scaled_two * mid_n, axis=1, keepdims=True)))
    d_mid_b = d_mid.astype(jnp.bfloat16)
    d_attended = jnp.dot(d_mid_b, w_output.T, preferred_element_type=jnp.float32).astype(jnp.bfloat16)
    g_output = jnp.dot(attended.T, d_mid_b, preferred_element_type=jnp.float32)
    scores, grouped = scores_of(query_rot, key_rot, visible)
    probs32 = jnp.exp(scores - log_total)
    probs = probs32.astype(jnp.bfloat16)
    d_heads = d_attended.reshape(count, HK, HQ // HK, HD)
    d_probs = multiply('qkgd,skd->kgqs', d_heads, value_b)
    inner = lax.optimization_barrier(jnp.sum(probs32 * d_probs, axis=-1, keepdims=True))
    d_scores = (probs32 * (d_probs - inner) * HD ** (-0.5)).astype(jnp.bfloat16)
    d_value = multiply('kgqs,qkgd->skd', probs, d_heads)
    d_query = multiply('kgqs,skd->qkgd', d_scores, key_rot).reshape(count, HQ, HD)
    d_key = multiply('kgqs,qkgd->skd', d_scores, grouped)
    d_query = unrotate(d_query, cosine, sine).reshape(count, HQ * HD).astype(jnp.bfloat16)
    d_key = unrotate(d_key, cosine, sine).reshape(count, HK * HD).astype(jnp.bfloat16)
    d_value = d_value.reshape(count, HK * HD).astype(jnp.bfloat16)
    g_query = jnp.dot(normed_one.T, d_query, preferred_element_type=jnp.float32)
    g_key = jnp.dot(normed_one.T, d_key, preferred_element_type=jnp.float32)
    g_value = jnp.dot(normed_one.T, d_value, preferred_element_type=jnp.float32)
    d_normed_one = jnp.dot(d_query, w_query.T, preferred_element_type=jnp.float32) + jnp.dot(d_key, w_key.T, preferred_element_type=jnp.float32) + jnp.dot(d_value, w_value.T, preferred_element_type=jnp.float32)
    base_n = base * scale_one
    g_gain_attn = lax.optimization_barrier(jnp.sum(d_normed_one * base_n, axis=0))
    scaled_one = d_normed_one * gain_attn.astype(jnp.float32)
    d_base = d_mid + scale_one * (scaled_one - base_n * lax.optimization_barrier(jnp.mean(scaled_one * base_n, axis=1, keepdims=True)))
    return (d_base, (g_query, g_key, g_value, g_output, g_gate, g_up, g_down, g_gain_attn, g_gain_ffn))

def reference(hidden_in, cotangent, segment_ids, w_query, w_key, w_value, w_output, w_gate, w_up, w_down, gain_attn, gain_ffn):
    weights = (w_query, w_key, w_value, w_output, w_gate, w_up, w_down, gain_attn, gain_ffn)
    start = tuple((jnp.zeros(w.shape, jnp.float32) for w in weights))

    def step(carry, item):
        tokens, upstream, segments = item
        result, saved = forward(tokens, segments, weights)
        d_base, grads = backward(upstream, saved, weights)
        carry = tuple((a + b for a, b in zip(carry, grads)))
        return (carry, (result, d_base))
    totals, (outputs, d_inputs) = lax.scan(step, start, (hidden_in, cotangent, segment_ids))
    return (outputs, d_inputs, totals[0], totals[1], totals[2], totals[3], totals[4], totals[5], totals[6], totals[7], totals[8])
```

```python
import jax
import jax.numpy as jnp
from jax import lax
from jax.experimental import pallas as pl
from jax.experimental.pallas import tpu as pltpu
from jax.sharding import PartitionSpec as P

HQ = 15
HK = 5
HD = 64
EPS = 1e-05
THETA = 100000.0
F32 = jnp.float32
BF16 = jnp.bfloat16


def dot(a, b, dims=((1,), (0,)), out=F32):
    res = lax.dot_general(a, b, (dims, ((), ())), preferred_element_type=F32)
    return res.astype(out)


def multiply(form, left, right):
    return jnp.einsum(form, left, right, preferred_element_type=F32)


class Grid:
    def __init__(self, dp, fs):
        nc = 2 if dp % 2 == 0 else 1
        ny = dp // nc
        nx = ny if fs % ny == 0 else 1
        self.size = {"y": ny, "c": nc, "z": fs // nx, "x": nx}

    def where(self):
        d, f = lax.axis_index("dp"), lax.axis_index("fsdp")
        nc, nx = self.size["c"], self.size["x"]
        return {"y": d // nc, "c": d % nc, "z": f // nx, "x": f % nx}

    def pull(self, value, axis, k):
        n = self.size[axis]
        k %= n
        if k == 0:
            return value
        name = "dp" if axis in "yc" else "fsdp"
        hi, lo = ("y", "c") if axis in "yc" else ("z", "x")
        perm = []
        for i in range(self.size[hi]):
            for j in range(self.size[lo]):
                si, sj = ((i + k) % n, j) if axis == hi else (i, (j + k) % n)
                perm.append((si * self.size[lo] + sj, i * self.size[lo] + j))
        return lax.ppermute(value, name, perm)

    def push(self, value, axis, k):
        return self.pull(value, axis, -k)


def turn(array, shift, axis):
    n = array.shape[axis]
    if n == 1:
        return array
    return lax.dynamic_slice_in_dim(
        jnp.concatenate([array, array], axis), (n - shift) % n, n, axis
    )


def pick(array, index, axis):
    return lax.dynamic_index_in_dim(array, index, axis, keepdims=False)


def place(grid, at, parts, over):
    nz, nx = grid.size["z"], grid.size["x"]
    ny, nc = (grid.size["y"], grid.size["c"]) if over else (1, 1)
    rows, cols = parts[0][0][0].shape[1:]
    if rows % 8 == 0 and cols % 128 == 0 or rows % 8 == 0 and ny * nc == 1:
        spots = jnp.stack([at["z"], at["x"], at["y"], at["c"]]).astype(jnp.int32)
        flat = [(dx, dy, dc) for dx in range(nx) for dy in range(ny) for dc in range(nc)]

        def kernel(spot, *refs):
            out = refs[-1]
            for (dx, dy, dc), ref in zip(flat, refs[:-1]):
                xi = lax.rem(spot[1] + dx, nx)
                if ny * nc == 1:
                    out[0, xi] = ref[0]
                else:
                    col = lax.rem(spot[2] + dy, ny) * nc + lax.rem(spot[3] + dc, nc)
                    out[0, xi, :, pl.ds(pl.multiple_of(col * cols, 128), cols)] = ref[0]

        wide = ny * nc * cols
        result = pl.pallas_call(
            kernel,
            out_shape=jax.ShapeDtypeStruct((nz, nx, rows, wide), parts[0][0][0].dtype),
            grid_spec=pltpu.PrefetchScalarGridSpec(
                num_scalar_prefetch=1,
                grid=(nz,),
                in_specs=[pl.BlockSpec((1, rows, cols), lambda k, s: (k, 0, 0)) for _ in flat],
                out_specs=pl.BlockSpec(
                    (1, nx, rows, wide), lambda k, s: (lax.rem(k + s[0], nz), 0, 0, 0)
                ),
            ),
            name="place",
        )(spots, *[parts[dx][dy][dc] for dx, dy, dc in flat])
        return result.reshape(nz * nx * rows, wide)
    full = jnp.stack([jnp.stack([jnp.stack(b) for b in a]) for a in parts])
    full = turn(full, at["x"], 0)
    if over:
        full = turn(turn(full, at["y"], 1), at["c"], 2)
    full = turn(full, at["z"], 3)
    return full.transpose(3, 0, 4, 1, 2, 5).reshape(nz * nx * rows, ny * nc * cols)


def gather_zx(grid, own):
    line = jnp.stack([grid.pull(own, "z", k) for k in range(grid.size["z"])])
    return [grid.pull(line, "x", k) for k in range(grid.size["x"])]


def gather_yc(grid, own):
    line = [grid.pull(own, "y", k) for k in range(grid.size["y"])]
    return [[grid.pull(v, "c", k) for k in range(grid.size["c"])] for v in line]


def stack_yc(parts):
    return jnp.stack([jnp.stack(row) for row in parts])


def scatter_yc(grid, blocks):
    ny, nc = grid.size["y"], grid.size["c"]
    total = blocks[:, 0].astype(F32)
    for k in range(1, nc):
        total = total + grid.push(blocks[:, k], "c", k).astype(F32)
    result = total[0]
    for k in range(1, ny):
        result = result + grid.push(total[k].astype(BF16), "y", k).astype(F32)
    return result


def scatter_zx(grid, at, terms):
    nz, nx = grid.size["z"], grid.size["x"]
    terms = terms.reshape(nz, nx, terms.shape[0] // (nz * nx), terms.shape[1])
    total = pick(terms, at["x"], 1).astype(F32)
    for k in range(1, nx):
        sent = pick(terms, (at["x"] + k) % nx, 1)
        total = total + grid.push(sent, "x", k).astype(F32)
    total = total.astype(BF16)
    result = pick(total, at["z"], 0).astype(F32)
    for k in range(1, nz):
        sent = pick(total, (at["z"] + k) % nz, 0)
        result = result + grid.push(sent, "z", k).astype(F32)
    return result


def share_yc(grid, at, own):
    full = stack_yc(gather_yc(grid, own.astype(BF16)))
    full = turn(turn(full, at["y"], 0), at["c"], 1)
    return full.reshape(-1, *own.shape)


def swap_yc(grid, at, wide):
    ny, nc = grid.size["y"], grid.size["c"]
    cols = wide.shape[1] // (ny * nc)

    def block(dy, dc):
        rank = (at["y"] + dy) % ny * nc + (at["c"] + dc) % nc
        return lax.dynamic_slice_in_dim(wide, rank * cols, cols, 1)

    from_c = [
        grid.push(jnp.stack([block(dy, dc) for dy in range(ny)]), "c", dc) for dc in range(nc)
    ]
    both = jnp.stack(from_c, 1)
    got = [grid.push(both[dy], "y", dy) for dy in range(ny)]
    full = jnp.stack([got[(ny - dy) % ny] for dy in range(ny)])
    return jnp.stack([full[:, (nc - dc) % nc] for dc in range(nc)], 1)


def tables(segments):
    count = segments.shape[0]
    index = jnp.arange(count, dtype=jnp.int32)
    same = segments[None, :] == segments[:, None]
    earlier = same & (index[None, :] < index[:, None])
    position = jnp.sum(earlier.astype(F32), axis=1)
    freqs = THETA ** (-jnp.arange(HD // 2).astype(F32) * 2.0 / HD)
    angle = position[:, None] * freqs[None, :]
    visible = same & (index[None, :] <= index[:, None])
    return (jnp.cos(angle), jnp.sin(angle), visible)


def rotate(field, cosine, sine):
    half = field.shape[-1] // 2
    first, second = (field[..., :half], field[..., half:])
    cosine, sine = (cosine[:, None, :], sine[:, None, :])
    return jnp.concatenate(
        [first * cosine - second * sine, second * cosine + first * sine], axis=-1
    )


def unrotate(field, cosine, sine):
    return rotate(field, cosine, -sine)


def scores_of(query_rot, key_rot, visible):
    count = query_rot.shape[0]
    grouped = query_rot.reshape(count, HK, HQ // HK, HD)
    scores = multiply("qkgd,skd->kgqs", grouped, key_rot) * HD ** (-0.5)
    return (jnp.where(visible[None, None], scores, -1e30), grouped)


def attend(projected, segments):
    count = projected.shape[0]
    dq, dk = HQ * HD, HK * HD
    query = projected[:, :dq].reshape(count, HQ, HD)
    key = projected[:, dq : dq + dk].reshape(count, HK, HD)
    value = projected[:, dq + dk : dq + 2 * dk].reshape(count, HK, HD)
    cosine, sine, visible = tables(segments)
    query_rot = rotate(query, cosine, sine).astype(BF16)
    key_rot = rotate(key, cosine, sine).astype(BF16)
    value_b = value.astype(BF16)
    scores, grouped = scores_of(query_rot, key_rot, visible)
    top = jnp.max(scores, axis=-1, keepdims=True)
    expo = jnp.exp(scores - top)
    total = jnp.sum(expo, axis=-1, keepdims=True)
    log_total = top + jnp.log(total)
    probs = (expo / total).astype(BF16)
    attended = multiply("kgqs,skd->qkgd", probs, value_b).reshape(count, dq).astype(BF16)
    return attended, (query_rot, key_rot, value_b, log_total, cosine, sine, visible)


def attend_back(d_attended, saved):
    query_rot, key_rot, value_b, log_total, cosine, sine, visible = saved
    count = d_attended.shape[0]
    scores, grouped = scores_of(query_rot, key_rot, visible)
    probs32 = jnp.exp(scores - log_total)
    probs = probs32.astype(BF16)
    d_heads = d_attended.reshape(count, HK, HQ // HK, HD)
    d_probs = multiply("qkgd,skd->kgqs", d_heads, value_b)
    inner = jnp.sum(probs32 * d_probs, axis=-1, keepdims=True)
    d_scores = (probs32 * (d_probs - inner) * HD ** (-0.5)).astype(BF16)
    d_value = multiply("kgqs,qkgd->skd", probs, d_heads)
    d_query = multiply("kgqs,skd->qkgd", d_scores, key_rot).reshape(count, HQ, HD)
    d_key = multiply("kgqs,qkgd->skd", d_scores, grouped)
    d_query = unrotate(d_query, cosine, sine).reshape(count, HQ * HD).astype(BF16)
    d_key = unrotate(d_key, cosine, sine).reshape(count, HK * HD).astype(BF16)
    d_value = d_value.reshape(count, HK * HD).astype(BF16)
    return jnp.concatenate([d_query, d_key, d_value], axis=1)


def shards(
    grid,
    hidden_in,
    cotangent,
    segment_ids,
    w_query,
    w_key,
    w_value,
    w_output,
    w_gate,
    w_up,
    w_down,
    gain_attn,
    gain_ffn,
):
    at = grid.where()
    ny, nc = grid.size["y"], grid.size["c"]
    ranks = ny * nc
    fs = grid.size["z"] * grid.size["x"]
    rank = at["y"] * nc + at["c"]
    rows, hidden = w_gate.shape
    dq, dk = HQ * HD, HK * HD
    dqkv = dq + 2 * dk
    width = dqkv + dq

    gain_one = gain_attn.astype(F32)[:, None]
    gain_two = gain_ffn.astype(F32)[:, None]
    w_qkv = jnp.concatenate([w_query, w_key, w_value], axis=1)
    own_attn = jnp.concatenate([(w_qkv.astype(F32) * gain_one).astype(BF16), w_output.T], axis=1)
    own_attn = lax.dynamic_slice_in_dim(own_attn, rank * (width // ranks), width // ranks, 1)
    each = hidden // fs // ranks

    def units(w):
        w = pick(w.reshape(rows, fs, ranks, each), rank, 2).reshape(rows, fs * each)
        return (w.astype(F32) * gain_two).astype(BF16)

    own_gu = jnp.concatenate([units(w_gate), units(w_up)], axis=1)
    own_down = pick(w_down.reshape(ranks, each, w_down.shape[1]), rank, 0)

    tokens, upstream = hidden_in[0], cotangent[0]
    count, model = tokens.shape

    with jax.named_scope("gather_attn"):
        line = jnp.stack([grid.pull(own_attn, "z", k) for k in range(grid.size["z"])])
        parts = [gather_yc(grid, grid.pull(line, "x", k)) for k in range(grid.size["x"])]
        w_attn = place(grid, at, parts, True)
    with jax.named_scope("gather_ffn"):
        own_gu, own_down, _ = lax.optimization_barrier((own_gu, own_down, line))
        w_gu = place(grid, at, [[[v]] for v in gather_zx(grid, own_gu)], False)
        w_d = place(grid, at, [[[v]] for v in gather_zx(grid, own_down)], False)
    with jax.named_scope("gather_tokens"):
        upstream_all = stack_yc(gather_yc(grid, upstream)).reshape(-1, model)

    base = tokens.astype(F32)
    scale_one = lax.rsqrt(jnp.mean(base * base, axis=1, keepdims=True) + EPS)
    base_n = base * scale_one
    normed_one = base_n.astype(BF16)
    projected = dot(normed_one, w_attn)
    attended, saved = attend(projected, segment_ids[0])
    padded = jnp.concatenate([jnp.zeros((count, dqkv), BF16), attended], axis=1)
    mid = base + dot(padded, w_attn, ((1,), (1,)))
    scale_two = lax.rsqrt(jnp.mean(mid * mid, axis=1, keepdims=True) + EPS)
    mid_n = mid * scale_two
    normed_two = mid_n.astype(BF16)

    with jax.named_scope("gather_tokens"):
        tokens_two = stack_yc(gather_yc(grid, normed_two)).reshape(-1, model)
    inner = w_d.shape[0]
    gate_up = dot(tokens_two, w_gu)
    gate_pre, up_pre = gate_up[:, :inner], gate_up[:, inner:]
    sigma = jax.nn.sigmoid(gate_pre)
    mixed = (gate_pre * sigma * up_pre).astype(BF16)
    d_mixed = dot(upstream_all, w_d, ((1,), (1,)))
    d_gate = (d_mixed * up_pre * sigma * (1.0 + gate_pre * (1.0 - sigma))).astype(BF16)
    d_up = (d_mixed * gate_pre * sigma).astype(BF16)
    d_gate_up = jnp.concatenate([d_gate, d_up], axis=1)
    d_two = dot(d_gate_up, w_gu, ((1,), (1,)), BF16)
    with jax.named_scope("return_tokens"):
        scaled_two = scatter_yc(grid, d_two.reshape(ny, nc, count, model))
    part_out = dot(mixed, w_d, out=BF16)
    with jax.named_scope("return_tokens"):
        result = mid + scatter_yc(grid, part_out.reshape(ny, nc, count, model))
    result = result.astype(BF16)
    g_gu = dot(tokens_two, d_gate_up, ((0,), (0,)), BF16)
    g_d = dot(mixed, upstream_all, ((0,), (0,)), BF16)
    with jax.named_scope("reduce_ffn"):
        s_gu = scatter_zx(grid, at, g_gu)
        s_d = scatter_zx(grid, at, g_d)
        all_gu = share_yc(grid, at, s_gu).astype(F32)
        all_d = share_yc(grid, at, s_d).astype(F32)

    d_mid = upstream.astype(F32) + scale_two * (
        scaled_two - mid_n * jnp.mean(scaled_two * mid_n, axis=1, keepdims=True)
    )
    d_mid_b = d_mid.astype(BF16)
    d_attended = dot(d_mid_b, w_attn)[:, dqkv:].astype(BF16)
    d_qkv = attend_back(d_attended, saved)
    d_wide = jnp.concatenate([d_qkv, jnp.zeros((count, dq), BF16)], axis=1)
    scaled_one = dot(d_wide, w_attn, ((1,), (1,)))
    d_base = d_mid + scale_one * (
        scaled_one - base_n * jnp.mean(scaled_one * base_n, axis=1, keepdims=True)
    )

    with jax.named_scope("reduce_attn"):
        one_all = stack_yc(gather_yc(grid, normed_one)).reshape(-1, model)
        mid_all = stack_yc(gather_yc(grid, d_mid_b)).reshape(-1, model)
        right = swap_yc(grid, at, jnp.concatenate([d_qkv, attended], axis=1))
        right = right.reshape(ranks * count, width // ranks)
        first = rank * (width // ranks) + jnp.arange(width // ranks) < dqkv
        zero = jnp.zeros((), BF16)
        g_attn = dot(one_all, jnp.where(first, right, zero), ((0,), (0,)))
        g_attn = g_attn + dot(mid_all, jnp.where(first, zero, right), ((0,), (0,)))
        s_attn = scatter_zx(grid, at, g_attn.astype(BF16))
        all_attn = share_yc(grid, at, s_attn).astype(F32)

    g_all = all_attn.transpose(1, 0, 2).reshape(rows, width)
    g_q, g_k, g_v = (g_all[:, :dq], g_all[:, dq : dq + dk], g_all[:, dq + dk : dqkv])
    s_one = jnp.sum(g_all[:, :dqkv] * w_qkv.astype(F32), axis=1)
    g_out = g_all[:, dqkv:].T

    def whole(part):
        part = part.reshape(ranks, rows, fs, each).transpose(1, 2, 0, 3)
        return part.reshape(rows, hidden)

    g_gate, g_up = whole(all_gu[:, :, :inner]), whole(all_gu[:, :, inner:])
    s_two = jnp.sum(g_gate * w_gate.astype(F32) + g_up * w_up.astype(F32), axis=1)
    return (
        result[None],
        d_base[None],
        g_q * gain_one,
        g_k * gain_one,
        g_v * gain_one,
        g_out,
        g_gate * gain_two,
        g_up * gain_two,
        all_d.reshape(w_down.shape),
        s_one,
        s_two,
    )


def solution(mesh):
    grid = Grid(mesh.shape["dp"], mesh.shape["fsdp"])

    def step(*args):
        return shards(grid, *args)

    return jax.shard_map(
        step,
        mesh=mesh,
        in_specs=(
            P(("dp", "fsdp"), None, None),
            P(("dp", "fsdp"), None, None),
            P(("dp", "fsdp"), None),
            P("fsdp", None),
            P("fsdp", None),
            P("fsdp", None),
            P(None, "fsdp"),
            P("fsdp", None),
            P("fsdp", None),
            P("fsdp", None),
            P("fsdp"),
            P("fsdp"),
        ),
        out_specs=(
            P(("dp", "fsdp"), None, None),
            P(("dp", "fsdp"), None, None),
            P("fsdp", None),
            P("fsdp", None),
            P("fsdp", None),
            P(None, "fsdp"),
            P("fsdp", None),
            P("fsdp", None),
            P("fsdp", None),
            P("fsdp"),
            P("fsdp"),
        ),
        check_vma=False,
    )
```
